1024 devices in a mesh: dp: 32 (over z_lo, y), tensor: 32 (over z_hi, x, core).
Axes of the slice: x: 4, y: 8, z: 16 (z_hi: 4, z_lo: 4; z = z_hi * 4 + z_lo), core: 2. Of those that a mesh axis runs over, the one named last changes fastest.
Arguments:
- local_gate: bfloat16 [14336, 16384], P('tensor', 'dp'), may hold values from -6 to 6
- local_up: bfloat16 [14336, 16384], P('tensor', 'dp'), may hold values from -6 to 6
- local_grad: bfloat16 [16384, 4096], P('dp'), may hold values from -48 to 48
- orphan_gate: bfloat16 [14336, 1024], P('tensor', 'dp'), may hold values from -6 to 6
- orphan_up: bfloat16 [14336, 1024], P('tensor', 'dp'), may hold values from -6 to 6
- orphan_grad: bfloat16 [1024, 4096], P('dp'), may hold values from -48 to 48
- orphan_len: int32 [32], P('dp'), may hold values from 1 to 32, 896 in all
- orphan_dest: int32 [1024, 1], P('dp'), may hold values from 0 to 31; in each aligned block of 32 rows (0 to 31, 32 to 63, ...) at most 2 rows name the same one
- loop_order: int32 [32], replicated, may hold values from 0 to 31, each once
Outputs:
- down_grad: float32 [14336, 4096], P('tensor', 'dp')
- orphan_load: float32 [32], P('dp')
The draws below stay inside these ranges and needn't reach their ends.
Inputs may be any that keep to these rules, and one draw needn't show every extreme that they name: `orphan_dest`: among the 32 rows of one holder, at most 2 name the same replica, live or not, and some holder's rows reach 2 for some replica. `loop_order`: A permutation of the replicas.
All inputs are finite; a program needn't handle non-finite values. No bound on the sum of `orphan_len` on one device may be relied on, other than what follows from the above.
Results may differ from the reference program's by a relative error of at most 0.0041.
Values may be sent and summed in bfloat16 or wider, within the bound.
No kernel may reach another device: no remote copies, remote signals or barrier semaphores. Data moves between devices by JAX's collectives and lax.ppermute only.
A program may use at most 32 MiB of HBM per device.

```python
import math
import jax
import jax.numpy as jnp
import numpy as np

D = 4096
FF = 14336
LOC = 512
ORPH = 32
ROWS = 16384
ORPHANS = 1024
N_DP = 32


def raised(drawn, own_key, source, target, shards_of, factor):
    def block_of(position):
        return (jnp.arange(drawn.shape[position]) // (drawn.shape[position] // shards_of)).reshape((-1,) + (1,) * (drawn.ndim - 1 - position))

    near = jax.random.permutation(own_key, shards_of)[block_of(target)]
    far = (block_of(target) + shards_of // 2) % shards_of
    return jnp.where((block_of(source) == near) | (block_of(source) == far), factor * drawn, drawn)


def steps_of(key, shape, split, smallest, largest):
    gain = 1.0
    for position, parts in split:
        steps = jax.random.uniform(jax.random.fold_in(jax.random.fold_in(key, 6), position), (parts,), jnp.float32, smallest / len(split), largest / len(split))
        gain = gain * jnp.repeat(jnp.exp(steps), shape[position] // parts).reshape((-1,) + (1,) * (len(shape) - 1 - position))
    return gain


def profile(number_of, total, bound, lean):
    loads = [(1 << 20) // math.isqrt(standing ** lean) + 1 for standing in range(2, number_of + 1)]
    surplus, given = total - bound - (number_of - 1), [1] * (number_of - 1)
    while surplus > 0:
        free = [i for i in range(number_of - 1) if given[i] < bound]
        whole, left = sum([loads[i] for i in free]), surplus
        for i in free:
            extra = min(bound - given[i], max(1, left * loads[i] // whole), surplus)
            given[i] = given[i] + extra
            surplus = surplus - extra
    return np.array([bound] + given)


def ragged_sizes(rng, count, total, reach, skew):
    if count == 2:
        one = jax.random.randint(rng, (), max(1, total - reach), min(reach, total - 1) + 1)
        return jnp.stack([one, total - one])
    tallies = jnp.asarray(profile(count, total, reach, skew), jnp.int32)
    twos = (count - 1) // 2
    donor, taker = tallies[1:1 + 2 * twos:2], tallies[2:2 + 2 * twos:2]
    room = jnp.minimum(donor - 1, reach - taker)
    moved = jax.random.randint(jax.random.fold_in(rng, 1), (twos,), 0, 1 << 20) % (room + 1)
    tallies = tallies.at[1:1 + 2 * twos:2].set(donor - moved).at[2:2 + 2 * twos:2].set(taker + moved)
    return tallies[jax.random.permutation(jax.random.fold_in(rng, 2), count)]


def assign_block(own_key, own, number, rows, count, top, most, lean):
    order = jax.random.permutation(own_key, count)
    heavy_load, usual = portions_of(count, rows * top, most, lean, True), portions_of(count, rows * top, most, lean, False)
    places = jnp.arange(count)

    def named(tallies, turn):
        used = int((tallies > 0).sum())
        fixed = max(1, used // 4)
        shifted = fixed + (places - fixed + turn * (used - fixed)) % max(1, count - fixed)
        return jnp.zeros((count,), jnp.int32).at[order[jnp.where(places < fixed, places, shifted)]].set(jnp.asarray(tallies, jnp.int32))

    tallies = jnp.where(number % 4 == 0, named(heavy_load, number // 4), named(usual, number - number // 4 - 1))
    mixed = jax.random.permutation(jax.random.fold_in(own, 3), count)
    donor, sink = mixed[0:count // 2 * 2:2], mixed[1:count // 2 * 2:2]
    slack = jnp.minimum(tallies[donor] - 1, most - tallies[sink]) // 2
    slack = jnp.where((donor == order[0]) | (sink == order[0]) | (tallies[sink] == 0), 0, jnp.maximum(slack, 0))
    shifted = jax.random.randint(jax.random.fold_in(own, 4), (count // 2,), 0, 1 << 20) % (slack + 1)
    tallies = tallies.at[donor].add(-shifted).at[sink].add(shifted)
    labels = jnp.searchsorted(jnp.cumsum(tallies), jnp.arange(rows * top), side="right").astype(jnp.int32)
    table = labels.reshape(top, rows).T
    table = table[jax.random.permutation(jax.random.fold_in(own, 1), rows)]
    turn = jax.random.randint(jax.random.fold_in(own, 2), (rows, 1), 0, top)
    return jnp.take_along_axis(table, (jnp.arange(top)[None, :] + turn) % top, axis=1)


def portions_of(number_of, total, most, skew, full):
    weights = [(1 << 20) // math.isqrt(standing ** skew) + 1 for standing in range(1, number_of + 1)]
    largest = most if full else min(most, max(-(-total // number_of), total * weights[0] // sum(weights)))
    least = 1 if total - largest >= number_of - 1 else 0
    given, surplus = [largest] + [least] * (number_of - 1), total - largest - least * (number_of - 1)
    while surplus > 0:
        free = [i for i in range(1, number_of) if given[i] < largest] or [i for i in range(1, number_of) if given[i] < most]
        whole, left = sum([weights[i] for i in free]), surplus
        for i in free:
            extra = min(most - given[i], max(1, left * weights[i] // whole), surplus)
            given[i] = given[i] + extra
            surplus = surplus - extra
    return np.array(given)


def scatter_about(own_key, extent, width, limit, split=(), held_as=jnp.bfloat16):
    values = jax.random.normal(own_key, extent, jnp.float32) * width
    if len(split) > 0:
        values = steps_of(own_key, extent, split, -0.22, 0.18) * values
    return jnp.clip(values, min=-limit, max=limit).astype(held_as)


def bell_draw_with(rng, shape, deviation, reach, shards, heavy, held_as=jnp.bfloat16):
    drawn = deviation * jax.random.normal(rng, shape, jnp.float32)
    if shards:
        drawn = drawn * steps_of(rng, shape, shards, -0.22, 0.18)
    return jnp.clip(raised(drawn, jax.random.fold_in(rng, 3), *heavy), -reach, reach).astype(held_as)


def setup_inputs(seed: int = 0) -> dict:
    seeds = jax.random.split(jax.random.key(seed), 10)
    local_gate = scatter_about(seeds[0], (FF, ROWS), 1.0, 6.0, ((0, 32), (1, 32)))
    local_up = scatter_about(seeds[1], (FF, ROWS), 1.0, 6.0, ((0, 32), (1, 32)))
    local_grad = bell_draw_with(seeds[2], (ROWS, D), 8.0, 48.0, ((0, 32),), (0, 1, 32, 2.75))
    orphan_gate = scatter_about(seeds[3], (FF, ORPHANS), 1.0, 6.0, ((0, 32), (1, 32)))
    orphan_up = scatter_about(seeds[4], (FF, ORPHANS), 1.0, 6.0, ((0, 32), (1, 32)))
    orphan_grad = scatter_about(seeds[5], (ORPHANS, D), 8.0, 48.0, ((0, 32),))
    orphan_len = ragged_sizes(seeds[6], N_DP, N_DP * ORPH * 7 // 8, ORPH, 2).astype(jnp.int32)
    orphan_dest_keys = jax.random.split(jax.random.fold_in(seeds[7], 1), ORPHANS // ORPH)
    orphan_dest_turns = jax.random.permutation(jax.random.fold_in(seeds[7], 3), ORPHANS // ORPH)
    orphan_dest = jax.vmap(lambda own, number: assign_block(jax.random.fold_in(seeds[7], 2), own, number, ORPH, N_DP, 1, 2 * ORPH // N_DP, 2))(orphan_dest_keys, orphan_dest_turns).reshape((ORPHANS, 1))
    loop_order = jax.random.permutation(seeds[8], N_DP).astype(jnp.int32)
    return dict(local_gate=local_gate, local_up=local_up, local_grad=local_grad, orphan_gate=orphan_gate, orphan_up=orphan_up, orphan_grad=orphan_grad, orphan_len=orphan_len, orphan_dest=orphan_dest, loop_order=loop_order)


def hidden_of(gate, upper):
    return (jax.nn.silu(gate.astype(jnp.float32)) * upper.astype(jnp.float32)).astype(jnp.bfloat16)


def reference(local_gate, local_up, local_grad, orphan_gate, orphan_up, orphan_grad, orphan_len, orphan_dest, loop_order):
    targets = orphan_dest[:, 0]
    row_ids = jnp.arange(N_DP * ORPH, dtype=jnp.int32)
    holders = row_ids // ORPH
    live_rows = ((row_ids % ORPH) < orphan_len[holders]).astype(jnp.float32)
    one_hot = (targets[:, None] == jnp.arange(N_DP, dtype=jnp.int32)[None, :]).astype(jnp.float32)
    live_per = jnp.sum(one_hot * live_rows[:, None], axis=0)
    weight = 1.0 / (LOC + live_per)
    own_factor = jnp.repeat(weight, LOC)
    own_scaled = (local_grad.astype(jnp.float32) * own_factor[:, None]).astype(jnp.bfloat16)
    orphan_factor = jnp.sum(one_hot * weight[None, :], axis=1) * live_rows
    orphan_scaled = (orphan_grad.astype(jnp.float32) * orphan_factor[:, None]).astype(jnp.bfloat16)
    own_hidden = hidden_of(local_gate, local_up)
    orphan_hidden = hidden_of(orphan_gate, orphan_up)
    grad_full = jnp.dot(own_hidden, own_scaled, preferred_element_type=jnp.float32)
    grad_full = grad_full + jnp.dot(orphan_hidden, orphan_scaled, preferred_element_type=jnp.float32)
    down_grad = grad_full.reshape(FF, N_DP, D // N_DP)[:, loop_order].reshape(FF, D)
    return down_grad, live_per / ORPH
```

```python
import jax
import jax.numpy as jnp
from jax import lax
from jax.experimental import pallas as pl
from jax.experimental.pallas import tpu as pltpu
from jax.sharding import Mesh
from jax.sharding import PartitionSpec as P

DP = ("dp_0", "dp_1")


def hidden_of(gate, upper):
    gate = gate.astype(jnp.float32)
    return gate / (1.0 + jnp.exp(-gate)) * upper.astype(jnp.float32)


def partial_kernel(
    order_ref,
    place_ref,
    len_ref,
    counts_ref,
    dest_ref,
    gate_ref,
    up_ref,
    orphan_gate_ref,
    orphan_up_ref,
    grad_ref,
    orphan_grad_ref,
    out_ref,
    hidden_ref,
):
    own_rows, _ = grad_ref.shape
    orphans = orphan_grad_ref.shape[0]
    replicas, _, cols = out_ref.shape
    hidden_ref[:, :own_rows] = hidden_of(gate_ref[...], up_ref[...]).astype(jnp.bfloat16)
    extra = hidden_of(orphan_gate_ref[...], orphan_up_ref[...])
    hidden_ref[:, own_rows:] = extra.T.astype(jnp.bfloat16)

    weights = 1.0 / (own_rows + jnp.sum(counts_ref[...], axis=0, keepdims=True))
    lanes = lax.broadcasted_iota(jnp.int32, (1, replicas), 1)
    own_weight = jnp.sum(jnp.where(lanes == place_ref[0], weights, 0.0), axis=1, keepdims=True)
    one_hot = (dest_ref[...] == lax.broadcasted_iota(jnp.int32, (orphans, replicas), 1)).astype(
        jnp.float32
    )
    live = (lax.broadcasted_iota(jnp.int32, (orphans, 1), 0) < len_ref[0]).astype(jnp.float32)
    factors = jnp.sum(one_hot * weights, axis=1, keepdims=True) * live

    def scaled_block(slot):
        at = pl.ds(pl.multiple_of(order_ref[slot] * cols, cols), cols)
        own = grad_ref[:, at].astype(jnp.float32) * own_weight
        extra = orphan_grad_ref[:, at].astype(jnp.float32) * factors
        return jnp.concatenate([own.astype(jnp.bfloat16), extra.astype(jnp.bfloat16)], axis=0)

    def step(pair, carry):
        left, right = 2 * pair, 2 * pair + 1
        both = jnp.concatenate([scaled_block(left), scaled_block(right)], axis=1)
        term = jnp.dot(hidden_ref[...], both, preferred_element_type=jnp.float32)
        out_ref[left] = term[:, :cols].astype(jnp.bfloat16)
        out_ref[right] = term[:, cols:].astype(jnp.bfloat16)
        return carry

    lax.fori_loop(0, replicas // 2, step, 0, unroll=2)


def partial_blocks(order, place, length, counts, dest, gate, up, o_gate, o_up, grad, o_grad):
    replicas = order.shape[0]
    rows, own_rows = gate.shape
    cols = grad.shape[1] // replicas
    orphans = o_grad.shape[0]
    smem = pl.BlockSpec(memory_space=pltpu.SMEM)
    vmem = pl.BlockSpec(memory_space=pltpu.VMEM)
    depth = own_rows + orphans
    return pl.pallas_call(
        partial_kernel,
        out_shape=jax.ShapeDtypeStruct((replicas, rows, cols), jnp.bfloat16),
        in_specs=[smem] * 3 + [vmem] * 8,
        out_specs=vmem,
        scratch_shapes=[pltpu.VMEM((rows, depth), jnp.bfloat16)],
        cost_estimate=pl.CostEstimate(
            flops=2 * rows * depth * grad.shape[1],
            bytes_accessed=2 * depth * grad.shape[1] + 2 * rows * grad.shape[1],
            transcendentals=rows * depth,
        ),
    )(order, place, length, counts, dest, gate, up, o_gate, o_up, grad, o_grad)


def per_device(
    local_gate,
    local_up,
    local_grad,
    orphan_gate,
    orphan_up,
    orphan_grad,
    orphan_len,
    orphan_dest,
    loop_order,
):
    replicas = lax.axis_size(DP)
    place = lax.axis_index(DP)
    orphans = orphan_grad.shape[0]
    live = jnp.arange(orphans, dtype=jnp.int32) < orphan_len[0]
    hits = (orphan_dest == jnp.arange(replicas, dtype=jnp.int32)[None, :]) & live[:, None]
    mine = jnp.sum(hits.astype(jnp.float32), axis=0)
    counts = jnp.broadcast_to(mine[None, None], (replicas, 1, replicas))
    counts = lax.all_to_all(counts, DP, split_axis=0, concat_axis=0, tiled=True)
    counts = counts.reshape(replicas, replicas)
    load = lax.dynamic_slice_in_dim(jnp.sum(counts, axis=0), place, 1) / orphans
    blocks = partial_blocks(
        loop_order,
        place.astype(jnp.int32).reshape(1),
        orphan_len,
        counts,
        orphan_dest,
        local_gate,
        local_up,
        orphan_gate.T,
        orphan_up.T,
        local_grad,
        orphan_grad,
    )
    blocks = lax.all_to_all(blocks, DP, split_axis=0, concat_axis=0, tiled=True)
    return jnp.sum(blocks.astype(jnp.float32), axis=0), load


def solution(mesh):
    torus = Mesh(mesh.devices.reshape(4, 8, mesh.shape["tensor"]), ("dp_0", "dp_1", "tensor"))
    return jax.shard_map(
        per_device,
        mesh=torus,
        in_specs=(
            P("tensor", DP),
            P("tensor", DP),
            P(DP, None),
            P("tensor", DP),
            P("tensor", DP),
            P(DP, None),
            P(DP),
            P(DP, None),
            P(),
        ),
        out_specs=(P("tensor", DP), P(DP)),
        check_vma=False,
    )
```

```python
import jax
import jax.numpy as jnp
from jax import lax
from jax.experimental import pallas as pl
from jax.experimental.pallas import tpu as pltpu
from jax.sharding import Mesh
from jax.sharding import PartitionSpec as P


DP = ("dp_0", "dp_1")
SMEM = pl.BlockSpec(memory_space=pltpu.SMEM)
VMEM = pl.BlockSpec(memory_space=pltpu.VMEM)


def room(mib):
    return pltpu.CompilerParams(vmem_limit_bytes=mib * 2**20)


def hidden_of(gate, upper):
    gate = gate.astype(jnp.float32)
    return gate / (1.0 + jnp.exp(-gate)) * upper.astype(jnp.float32)


def own_products(order, place, gate, up, o_gate, o_up, grad):
    rows, depth = gate.shape
    outer, inner = lax.axis_size("dp_0"), lax.axis_size("dp_1")
    cols = grad.shape[1] // (outer * inner)
    orphans = o_gate.shape[0]
    far = inner // 2

    def kernel(order_ref, place_ref, gate_ref, up_ref, o_gate_ref, o_up_ref, *refs):
        grad_refs, (far_ref, ring_ref, extra_ref, hidden_ref) = refs[:outer], refs[outer:]

        @pl.when(pl.program_id(0) == 0)
        def _():
            hidden_ref[...] = hidden_of(gate_ref[...], up_ref[...]).astype(jnp.bfloat16)
            extra_ref[...] = hidden_of(o_gate_ref[...], o_up_ref[...]).T.astype(jnp.bfloat16)

        for first in range(0, outer, 2):
            both = jnp.concatenate([grad_refs[first][...], grad_refs[first + 1][...]], axis=1)
            term = jnp.dot(hidden_ref[...], both, preferred_element_type=jnp.float32)
            for k in range(2):
                ring_ref[0, first + k] = term[:, k * cols : (k + 1) * cols]

        @pl.when(pl.program_id(0) == 0)
        def _():
            far_ref[...] = ring_ref[0]

    def column_block(z):
        def at(turn, order_ref, place_ref):
            away = turn + turn // far + far * (1 - jnp.minimum(turn, 1))
            return 0, order_ref[z * inner + lax.rem(place_ref[0] + away, inner)]

        return pl.BlockSpec((depth, cols), at)

    def whole(*shape):
        return pl.BlockSpec(shape, lambda turn, *_: (0,) * len(shape))

    return pl.pallas_call(
        kernel,
        name="own_products",
        out_shape=(
            jax.ShapeDtypeStruct((outer, rows, cols), jnp.float32),
            jax.ShapeDtypeStruct((inner - 1, outer, rows, cols), jnp.float32),
            jax.ShapeDtypeStruct((rows, orphans), jnp.bfloat16),
        ),
        grid_spec=pltpu.PrefetchScalarGridSpec(
            num_scalar_prefetch=2,
            grid=(inner,),
            in_specs=[whole(*gate.shape)] * 2
            + [whole(*o_gate.shape)] * 2
            + [column_block(z) for z in range(outer)],
            out_specs=(
                whole(outer, rows, cols),
                pl.BlockSpec(
                    (1, outer, rows, cols),
                    lambda turn, *_: (jnp.maximum(turn - 1, 0), 0, 0, 0),
                ),
                whole(rows, orphans),
            ),
            scratch_shapes=[pltpu.VMEM((rows, depth), jnp.bfloat16)],
        ),
        cost_estimate=pl.CostEstimate(
            flops=2 * rows * depth * grad.shape[1],
            bytes_accessed=2 * depth * grad.shape[1] + 4 * rows * grad.shape[1],
            transcendentals=rows * depth,
        ),
    )(order, place, gate, up, o_gate, o_up, *[grad] * outer)


def first_terms(order, place, length, counts, dest, o_grad, far_part, extra, own_rows):
    outer, inner = lax.axis_size("dp_0"), lax.axis_size("dp_1")
    replicas = outer * inner
    orphans = o_grad.shape[0]
    _, rows, cols = far_part.shape
    half, far = rows // 2, inner // 2

    def kernel(
        order_ref, place_ref, len_ref, counts_ref, dest_ref, grad_ref, far_ref, extra_ref,
        weight_ref, load_ref, out_ref, up_ref, down_ref,
    ):
        taken = jnp.sum(counts_ref[...], axis=0, keepdims=True)
        weights = 1.0 / (own_rows + taken)
        lanes = lax.broadcasted_iota(jnp.int32, (1, replicas), 1)
        mine = lanes == place_ref[1]
        load_ref[...] = jnp.sum(jnp.where(mine, taken, 0.0), axis=1, keepdims=True) / orphans
        own = jnp.sum(jnp.where(mine, weights, 0.0), axis=1, keepdims=True)
        weight_ref[...] = jnp.broadcast_to(own, weight_ref.shape)
        names = lax.broadcasted_iota(jnp.int32, (orphans, replicas), 1)
        one_hot = (dest_ref[...] == names).astype(jnp.float32)
        live = (lax.broadcasted_iota(jnp.int32, (orphans, 1), 0) < len_ref[0]).astype(jnp.float32)
        factors = jnp.sum(one_hot * weights, axis=1, keepdims=True) * live
        for away in range(inner):
            to = lax.rem(place_ref[0] + away, inner)
            for z in range(outer):
                at = pl.ds(pl.multiple_of(order_ref[z * inner + to] * cols, cols), cols)
                scaled = grad_ref[:, at].astype(jnp.float32) * factors
                out_ref[away, z] = scaled.astype(jnp.bfloat16)
        for z in range(outer):
            total = far_ref[z] * own + jnp.dot(
                extra_ref[...], out_ref[far, z], preferred_element_type=jnp.float32
            )
            up_ref[z] = total[:half].astype(jnp.bfloat16)
            down_ref[z] = total[half:].astype(jnp.bfloat16)

    return pl.pallas_call(
        kernel,
        name="first_terms",
        out_shape=(
            jax.ShapeDtypeStruct((1, cols), jnp.float32),
            jax.ShapeDtypeStruct((1, 1), jnp.float32),
            jax.ShapeDtypeStruct((inner, outer, orphans, cols), jnp.bfloat16),
            jax.ShapeDtypeStruct((outer, half, cols), jnp.bfloat16),
            jax.ShapeDtypeStruct((outer, rows - half, cols), jnp.bfloat16),
        ),
        in_specs=[SMEM] * 3 + [VMEM] * 5,
        out_specs=(VMEM,) * 5,
        compiler_params=room(6),
        cost_estimate=pl.CostEstimate(
            flops=2 * outer * rows * orphans * cols,
            bytes_accessed=4 * orphans * o_grad.shape[1] + 6 * outer * rows * cols,
            transcendentals=0,
        ),
    )(order, place, length, counts, dest, o_grad, far_part, extra)


def ring_sum(name, away, weight, ring, extra, o_scaled, received):
    _, outer, rows, cols = ring.shape
    inner, _, orphans, _ = o_scaled.shape
    at = (away - 1 - away // (inner // 2)) % inner if away else inner - 2

    def kernel(weight_ref, ring_ref, extra_ref, scaled_ref, *refs):
        *came, out_ref, own_ref, sem = refs
        copy = pltpu.make_async_copy(ring_ref.at[at], own_ref, sem)
        copy.start()
        copy.wait()
        for z in range(outer):
            total = own_ref[z] * weight_ref[...] + jnp.dot(
                extra_ref[...], scaled_ref[away, z], preferred_element_type=jnp.float32
            )
            for first in range(0, rows, rows // 2):
                part = total[first : first + rows // 2]
                for c, (_, start) in zip(came, received):
                    if start <= first < start + c.shape[1]:
                        within = first - start
                        part = part + c[z, within : within + rows // 2].astype(jnp.float32)
                out_ref[z, first : first + rows // 2] = part.astype(jnp.bfloat16)

    return pl.pallas_call(
        kernel,
        name=name,
        out_shape=jax.ShapeDtypeStruct((outer, rows, cols), jnp.bfloat16),
        in_specs=[VMEM, pl.BlockSpec(memory_space=pl.ANY)] + [VMEM] * (2 + len(received)),
        out_specs=VMEM,
        scratch_shapes=[pltpu.VMEM((outer, rows, cols), jnp.float32), pltpu.SemaphoreType.DMA],
        compiler_params=room(6),
        cost_estimate=pl.CostEstimate(
            flops=2 * outer * rows * orphans * cols,
            bytes_accessed=8 * outer * rows * cols,
            transcendentals=0,
        ),
    )(weight, ring, extra, o_scaled, *[a for a, _ in received])


def total_of(near):
    outer, rows, cols = near.shape

    def kernel(near_ref, out_ref):
        whole = near_ref[0].astype(jnp.float32)
        for k in range(1, outer):
            whole = whole + near_ref[k].astype(jnp.float32)
        out_ref[...] = whole

    return pl.pallas_call(
        kernel,
        name="total_of",
        out_shape=jax.ShapeDtypeStruct((rows, cols), jnp.float32),
        in_specs=[VMEM],
        out_specs=VMEM,
        compiler_params=room(4),
    )(near)


def shifted(array, by):
    size = lax.axis_size("dp_1")
    return lax.ppermute(array, "dp_1", [(i, (i + by) % size) for i in range(size)])


def exchanged(array, axis):
    return lax.all_to_all(array, axis, split_axis=0, concat_axis=0, tiled=True)


def per_device(
    local_gate,
    local_up,
    local_grad,
    orphan_gate,
    orphan_up,
    orphan_grad,
    orphan_len,
    orphan_dest,
    loop_order,
):
    replicas = lax.axis_size(DP)
    inner = lax.axis_size("dp_1")
    me = lax.axis_index(DP).astype(jnp.int32)
    place = jnp.stack([lax.axis_index("dp_1").astype(jnp.int32), me])
    orphans = orphan_grad.shape[0]
    live = jnp.arange(orphans, dtype=jnp.int32) < orphan_len[0]
    hits = (orphan_dest == jnp.arange(replicas, dtype=jnp.int32)[None, :]) & live[:, None]
    mine = jnp.sum(hits.astype(jnp.float32), axis=0)
    counts = exchanged(jnp.broadcast_to(mine[None, None], (replicas, 1, replicas)), DP)
    counts = counts.reshape(replicas, replicas)
    far_part, ring, extra = own_products(
        loop_order, place, local_gate, local_up, orphan_gate.T, orphan_up.T, local_grad
    )
    weight, load, o_scaled, up, down = first_terms(
        loop_order,
        place,
        orphan_len,
        counts,
        orphan_dest,
        orphan_grad,
        far_part,
        extra,
        local_grad.shape[0],
    )
    args = (weight, ring, extra, o_scaled)
    up, down = (shifted(up, 1), 0), (shifted(down, -1), up.shape[1])
    for away in range(inner // 2 - 1, 0, -1):
        up = shifted(ring_sum(f"up_{away}", away, *args, [up]), 1), 0
        down = shifted(ring_sum(f"down_{away}", inner - away, *args, [down]), -1), 0
    near = ring_sum("near", 0, *args, [up, down])
    return total_of(exchanged(near, "dp_0")), load.reshape(1)


def solution(mesh):
    torus = Mesh(mesh.devices.reshape(4, 8, mesh.shape["tensor"]), ("dp_0", "dp_1", "tensor"))
    return jax.shard_map(
        per_device,
        mesh=torus,
        in_specs=(
            P("tensor", DP),
            P("tensor", DP),
            P(DP, None),
            P("tensor", DP),
            P("tensor", DP),
            P(DP, None),
            P(DP),
            P(DP, None),
            P(),
        ),
        out_specs=(P("tensor", DP), P(DP)),
        check_vma=False,
    )
```

```python
import jax
import jax.numpy as jnp
from jax import lax
from jax.experimental import pallas as pl
from jax.experimental.pallas import tpu as pltpu
from jax.sharding import Mesh
from jax.sharding import PartitionSpec as P


DP = ("dp_0", "dp_1")
UP_ROWS = 256
SMEM = pl.BlockSpec(memory_space=pltpu.SMEM)
VMEM = pl.BlockSpec(memory_space=pltpu.VMEM)


def room(mib):
    return pltpu.CompilerParams(vmem_limit_bytes=mib * 2**20)


def hidden_of(gate, upper):
    gate = gate.astype(jnp.float32)
    return gate / (1.0 + jnp.exp(-gate)) * upper.astype(jnp.float32)


def first_message(order, place, gate, up, o_gate, o_up, grad, o_grad):
    rows, depth = gate.shape
    outer, inner = lax.axis_size("dp_0"), lax.axis_size("dp_1")
    cols = grad.shape[1] // (outer * inner)
    orphans = o_gate.shape[0]
    half, far = UP_ROWS, inner // 2

    def kernel(order_ref, place_ref, gate_ref, up_ref, o_gate_ref, o_up_ref, *refs):
        grad_refs, o_grad_refs = refs[:outer], refs[outer : 2 * outer]
        hidden_ref, *messages = refs[2 * outer :]
        hidden_ref[:, :depth] = hidden_of(gate_ref[...], up_ref[...]).astype(jnp.bfloat16)
        extra = hidden_of(o_gate_ref[...], o_up_ref[...])
        hidden_ref[:, depth:] = extra.T.astype(jnp.bfloat16)
        for first in range(0, outer, 2):
            both = jnp.concatenate([grad_refs[first][...], grad_refs[first + 1][...]], axis=1)
            term = jnp.dot(hidden_ref[:, :depth], both, preferred_element_type=jnp.float32)
            for k in range(2):
                part = term[:, k * cols : (k + 1) * cols].astype(jnp.bfloat16)
                messages[0][first + k, :half] = part[:half]
                messages[1][first + k, : rows - half] = part[half:]
        for message, start, stop in ((messages[0], 0, half), (messages[1], half, rows)):
            at = stop - start
            for z in range(outer):
                message[z, at : at + orphans] = o_grad_refs[z][...]
                piece = extra[:, min(start + z * cols, stop) : min(start + (z + 1) * cols, stop)]
                piece = piece.astype(jnp.bfloat16)
                if piece.shape[1] < cols:
                    gap = jnp.zeros((orphans, cols - piece.shape[1]), jnp.bfloat16)
                    piece = jnp.concatenate([piece, gap], axis=1) if piece.shape[1] else gap
                message[z, at + orphans :] = piece

    def column_block(height, z):
        def at(turn, order_ref, place_ref):
            return 0, order_ref[z * inner + lax.rem(place_ref[0] + far, inner)]

        return pl.BlockSpec((height, cols), at)

    def whole(*shape):
        return pl.BlockSpec(shape, lambda turn, *_: (0,) * len(shape))

    shapes = [
        (rows, depth + orphans),
        (outer, half + 2 * orphans, cols),
        (outer, rows - half + 2 * orphans, cols),
    ]
    return pl.pallas_call(
        kernel,
        name="first_message",
        out_shape=[jax.ShapeDtypeStruct(shape, jnp.bfloat16) for shape in shapes],
        grid_spec=pltpu.PrefetchScalarGridSpec(
            num_scalar_prefetch=2,
            grid=(1,),
            in_specs=[whole(*gate.shape)] * 2
            + [whole(*o_gate.shape)] * 2
            + [column_block(depth, z) for z in range(outer)]
            + [column_block(orphans, z) for z in range(outer)],
            out_specs=[whole(*shape) for shape in shapes],
        ),
        cost_estimate=pl.CostEstimate(
            flops=2 * rows * depth * outer * cols,
            bytes_accessed=8 * rows * depth,
            transcendentals=rows * depth,
        ),
    )(order, place, gate, up, o_gate, o_up, *[grad] * outer, *[o_grad] * outer)


def other_terms(order, place, names, hidden, grad, o_grad):
    rows, _ = hidden.shape
    own_rows, _ = grad.shape
    outer, inner = lax.axis_size("dp_0"), lax.axis_size("dp_1")
    replicas = outer * inner
    orphans = o_grad.shape[0]
    cols = grad.shape[1] // replicas

    def kernel(
        order_ref, place_ref, names_ref, hidden_ref, grad_ref, o_grad_ref,
        ring_ref, weight_ref, load_ref, up_ref, down_ref,
    ):
        names = names_ref[...].T
        lanes = lax.broadcasted_iota(jnp.int32, (orphans, replicas), 1)
        marks = lanes.astype(jnp.float32)
        taken = jnp.zeros((orphans, replicas), jnp.float32)
        for holder in range(replicas):
            taken = taken + (names[:, holder : holder + 1] == marks).astype(jnp.float32)
        taken = jnp.sum(taken, axis=0, keepdims=True)
        weights = 1.0 / (own_rows + taken)
        line = place_ref[1] - place_ref[0]
        holders = [
            place_ref[1],
            line + lax.rem(place_ref[0] + inner - 1, inner),
            line + lax.rem(place_ref[0] + 1, inner),
        ]

        def entry(row, holder):
            return jnp.sum(jnp.where(lanes[:1] == holder, row, 0.0), axis=1, keepdims=True)

        load_ref[...] = entry(taken, holders[0]) / orphans
        factors = []
        for k, holder in enumerate(holders):
            weight_ref[k : k + 1] = jnp.broadcast_to(entry(weights, holder), (1, cols))
            column = jnp.sum(jnp.where(lanes == holder, names, 0.0), axis=1, keepdims=True)
            factors.append(
                jnp.sum(jnp.where(column == marks, weights, 0.0), axis=1, keepdims=True)
            )
        up_ref[...] = jnp.broadcast_to(factors[1], up_ref.shape)
        down_ref[...] = jnp.broadcast_to(factors[2], down_ref.shape)
        own_weight = weight_ref[:1]

        for turn in range(inner - 1):
            away = turn + 1 + (turn + 1) // (inner // 2)
            to = lax.rem(place_ref[0] + away, inner)

            def block(z):
                at = pl.ds(pl.multiple_of(order_ref[z * inner + to] * cols, cols), cols)
                own = grad_ref[:, at].astype(jnp.float32) * own_weight
                extra = o_grad_ref[:, at].astype(jnp.float32) * factors[0]
                return jnp.concatenate([own.astype(jnp.bfloat16), extra.astype(jnp.bfloat16)], axis=0)

            for first in range(0, outer, 2):
                both = jnp.concatenate([block(first), block(first + 1)], axis=1)
                term = jnp.dot(hidden_ref[...], both, preferred_element_type=jnp.float32)
                for k in range(2):
                    ring_ref[turn, first + k] = term[:, k * cols : (k + 1) * cols]

    return pl.pallas_call(
        kernel,
        name="other_terms",
        out_shape=(
            jax.ShapeDtypeStruct((inner - 1, outer, rows, cols), jnp.float32),
            jax.ShapeDtypeStruct((3, cols), jnp.float32),
            jax.ShapeDtypeStruct((1, 1), jnp.float32),
            jax.ShapeDtypeStruct((orphans, cols), jnp.float32),
            jax.ShapeDtypeStruct((orphans, cols), jnp.float32),
        ),
        in_specs=[SMEM] * 2 + [VMEM] * 4,
        out_specs=(VMEM,) * 5,
        compiler_params=room(20),
        cost_estimate=pl.CostEstimate(
            flops=2 * rows * hidden.shape[1] * grad.shape[1],
            bytes_accessed=2 * hidden.shape[1] * grad.shape[1] + 4 * rows * grad.shape[1],
            transcendentals=0,
        ),
    )(order, place, names, hidden, grad, o_grad)


def ring_sum(away, ring, received, first=None):
    inner, outer, rows, cols = ring.shape[0] + 1, *ring.shape[1:]
    at = (away - 1 - away // (inner // 2)) % inner if away else inner - 2
    operands = [*received, *([] if first is None else [first[0], first[2]])]

    def kernel(ring_ref, *refs):
        came, (out_ref, own_ref, sem) = refs[: len(operands)], refs[len(operands) :]
        copy = pltpu.make_async_copy(ring_ref.at[at], own_ref, sem)
        copy.start()
        if first is not None:
            message, weight_ref, factor_ref = came
            orphans = factor_ref.shape[0]
            count = message.shape[1] - 2 * orphans
            pieces = [message[z, count + orphans :] for z in range(-(-count // cols))]
            theirs = jnp.concatenate(pieces, axis=1).astype(jnp.float32).T
            theirs = theirs[:count].astype(jnp.bfloat16)
        copy.wait()
        for z in range(outer):
            if first is None:
                total = own_ref[z]
                for c in came:
                    total = total + c[z].astype(jnp.float32)
                out_ref[z] = total.astype(jnp.bfloat16)
                continue
            _, row, _, start = first
            scaled = message[z, count : count + orphans].astype(jnp.float32) * factor_ref[...]
            part = message[z, :count].astype(jnp.float32) * weight_ref[row : row + 1]
            part = part + jnp.dot(
                theirs, scaled.astype(jnp.bfloat16), preferred_element_type=jnp.float32
            )
            out_ref[z] = own_ref[z].astype(jnp.bfloat16)
            part = own_ref[z, start : start + count] + part
            out_ref[z, start : start + count] = part.astype(jnp.bfloat16)

    return pl.pallas_call(
        kernel,
        out_shape=jax.ShapeDtypeStruct((outer, rows, cols), jnp.bfloat16),
        in_specs=[pl.BlockSpec(memory_space=pl.ANY)] + [VMEM] * len(operands),
        out_specs=VMEM,
        scratch_shapes=[pltpu.VMEM((outer, rows, cols), jnp.float32), pltpu.SemaphoreType.DMA],
        compiler_params=room(6),
        cost_estimate=pl.CostEstimate(
            flops=2 * outer * rows * cols,
            bytes_accessed=8 * outer * rows * cols,
            transcendentals=0,
        ),
    )(ring, *operands)


def total_of(near):
    outer, rows, cols = near.shape

    def kernel(near_ref, out_ref):
        whole = near_ref[0].astype(jnp.float32)
        for k in range(1, outer):
            whole = whole + near_ref[k].astype(jnp.float32)
        out_ref[...] = whole

    return pl.pallas_call(
        kernel,
        name="total_of",
        out_shape=jax.ShapeDtypeStruct((rows, cols), jnp.float32),
        in_specs=[VMEM],
        out_specs=VMEM,
        compiler_params=room(4),
    )(near)


def shifted(array, by):
    size = lax.axis_size("dp_1")
    return lax.ppermute(array, "dp_1", [(i, (i + by) % size) for i in range(size)])


def exchanged(array, axis):
    return lax.all_to_all(array, axis, split_axis=0, concat_axis=0, tiled=True)


def per_device(
    local_gate,
    local_up,
    local_grad,
    orphan_gate,
    orphan_up,
    orphan_grad,
    orphan_len,
    orphan_dest,
    loop_order,
):
    replicas = lax.axis_size(DP)
    inner = lax.axis_size("dp_1")
    me = lax.axis_index(DP).astype(jnp.int32)
    place = jnp.stack([lax.axis_index("dp_1").astype(jnp.int32), me])
    orphans = orphan_grad.shape[0]
    live = jnp.arange(orphans, dtype=jnp.int32) < orphan_len[0]
    names = jnp.where(live, orphan_dest[:, 0], -1).astype(jnp.float32)
    names = jnp.broadcast_to(names[None, None], (replicas, 1, orphans))
    names = exchanged(names, DP)
    hidden, up, down = first_message(
        loop_order,
        place,
        local_gate,
        local_up,
        orphan_gate.T,
        orphan_up.T,
        local_grad,
        orphan_grad,
    )
    up, down = shifted(up, 1), shifted(down, -1)
    ring, weight, load, up_factor, down_factor = other_terms(
        loop_order, place, names.reshape(replicas, orphans), hidden, local_grad, orphan_grad
    )
    ups, downs = (weight, 1, up_factor, 0), (weight, 2, down_factor, UP_ROWS)
    for away in range(inner // 2 - 1, 0, -1):
        up = shifted(ring_sum(away, ring, [up], ups), 1)
        down = shifted(ring_sum(inner - away, ring, [down], downs), -1)
        ups = downs = None
    near = ring_sum(0, ring, [up, down])
    return total_of(exchanged(near, "dp_0")), load.reshape(1)


def solution(mesh):
    torus = Mesh(mesh.devices.reshape(4, 8, mesh.shape["tensor"]), ("dp_0", "dp_1", "tensor"))

    return jax.shard_map(
        per_device,
        mesh=torus,
        in_specs=(
            P("tensor", DP),
            P("tensor", DP),
            P(DP, None),
            P("tensor", DP),
            P("tensor", DP),
            P(DP, None),
            P(DP),
            P(DP, None),
            P(),
        ),
        out_specs=(P("tensor", DP), P(DP)),
        check_vma=False,
    )
```

```python
import jax
import jax.numpy as jnp
from jax import lax
from jax.experimental import pallas as pl
from jax.experimental.pallas import tpu as pltpu
from jax.sharding import Mesh
from jax.sharding import PartitionSpec as P


DP = ("dp_0", "dp_1")
UP_ROWS = 256
SMEM = pl.BlockSpec(memory_space=pltpu.SMEM)
VMEM = pl.BlockSpec(memory_space=pltpu.VMEM)


def room(mib):
    return pltpu.CompilerParams(vmem_limit_bytes=mib * 2**20)


def hidden_of(gate, upper):
    gate = gate.astype(jnp.float32)
    return gate / (1.0 + jnp.exp(-gate)) * upper.astype(jnp.float32)


def first_message(order, place, gate, up, o_gate, o_up, grad, o_grad):
    rows, depth = gate.shape
    outer, inner = lax.axis_size("dp_0"), lax.axis_size("dp_1")
    cols = grad.shape[1] // (outer * inner)
    orphans = o_gate.shape[0]
    half, far = UP_ROWS, inner // 2

    def kernel(order_ref, place_ref, gate_ref, up_ref, o_gate_ref, o_up_ref, *refs):
        grad_refs, o_grad_refs = refs[:outer], refs[outer : 2 * outer]
        hidden_ref, *messages = refs[2 * outer :]
        hidden_ref[:, :depth] = hidden_of(gate_ref[...], up_ref[...]).astype(jnp.bfloat16)
        extra = hidden_of(o_gate_ref[...], o_up_ref[...])
        hidden_ref[:, depth:] = extra.T.astype(jnp.bfloat16)
        for first in range(0, outer, 2):
            both = jnp.concatenate([grad_refs[first][...], grad_refs[first + 1][...]], axis=1)
            term = jnp.dot(hidden_ref[:, :depth], both, preferred_element_type=jnp.float32)
            for k in range(2):
                part = term[:, k * cols : (k + 1) * cols].astype(jnp.bfloat16)
                messages[0][first + k, :half] = part[:half]
                messages[1][first + k, : rows - half] = part[half:]
        for message, start, stop in ((messages[0], 0, half), (messages[1], half, rows)):
            at = stop - start
            for z in range(outer):
                message[z, at : at + orphans] = o_grad_refs[z][...]
                left = start + z % (outer // 2) * cols
                piece = extra[:, left : min(left + cols, stop)]
                piece = piece.astype(jnp.bfloat16)
                if piece.shape[1] < cols:
                    gap = jnp.zeros((orphans, cols - piece.shape[1]), jnp.bfloat16)
                    piece = jnp.concatenate([piece, gap], axis=1)
                message[z, at + orphans :] = piece

    def column_block(height, z):
        def at(turn, order_ref, place_ref):
            return 0, order_ref[z * inner + lax.rem(place_ref[0] + far, inner)]

        return pl.BlockSpec((height, cols), at)

    def whole(*shape):
        return pl.BlockSpec(shape, lambda turn, *_: (0,) * len(shape))

    shapes = [
        (rows, depth + orphans),
        (outer, half + 2 * orphans, cols),
        (outer, rows - half + 2 * orphans, cols),
    ]
    return pl.pallas_call(
        kernel,
        name="first_message",
        out_shape=[jax.ShapeDtypeStruct(shape, jnp.bfloat16) for shape in shapes],
        grid_spec=pltpu.PrefetchScalarGridSpec(
            num_scalar_prefetch=2,
            grid=(1,),
            in_specs=[whole(*gate.shape)] * 2
            + [whole(*o_gate.shape)] * 2
            + [column_block(depth, z) for z in range(outer)]
            + [column_block(orphans, z) for z in range(outer)],
            out_specs=[whole(*shape) for shape in shapes],
        ),
        cost_estimate=pl.CostEstimate(
            flops=2 * rows * depth * outer * cols,
            bytes_accessed=8 * rows * depth,
            transcendentals=rows * depth,
        ),
    )(order, place, gate, up, o_gate, o_up, *[grad] * outer, *[o_grad] * outer)


def other_terms(order, place, me, names, hidden, grad, o_grad):
    rows, _ = hidden.shape
    own_rows, _ = grad.shape
    outer, inner = lax.axis_size("dp_0"), lax.axis_size("dp_1")
    replicas = outer * inner
    orphans = o_grad.shape[0]
    cols = grad.shape[1] // replicas

    def kernel(
        order_ref, place_ref, me_ref, names_ref, hidden_ref, grad_ref, o_grad_ref,
        ring_ref, weight_ref, load_ref, up_ref, down_ref,
    ):
        names = names_ref[...].T
        lanes = lax.broadcasted_iota(jnp.int32, (orphans, replicas), 1)
        marks = lanes.astype(jnp.float32)
        taken = jnp.zeros((orphans, replicas), jnp.float32)
        for holder in range(replicas):
            taken = taken + (names[:, holder : holder + 1] == marks).astype(jnp.float32)
        taken = jnp.sum(taken, axis=0, keepdims=True)
        weights = 1.0 / (own_rows + taken)
        line = me_ref[0] - place_ref[0]
        holders = [
            me_ref[0],
            line + lax.rem(place_ref[0] + inner - 1, inner),
            line + lax.rem(place_ref[0] + 1, inner),
        ]

        def entry(row, holder):
            return jnp.sum(jnp.where(lanes[:1] == holder, row, 0.0), axis=1, keepdims=True)

        load_ref[...] = entry(taken, holders[0]) / orphans
        factors = []
        for k, holder in enumerate(holders):
            weight_ref[k : k + 1] = jnp.broadcast_to(entry(weights, holder), (1, cols))
            column = jnp.sum(jnp.where(lanes == holder, names, 0.0), axis=1, keepdims=True)
            factors.append(
                jnp.sum(jnp.where(column == marks, weights, 0.0), axis=1, keepdims=True)
            )
        up_ref[...] = jnp.broadcast_to(factors[1], up_ref.shape)
        down_ref[...] = jnp.broadcast_to(factors[2], down_ref.shape)
        own_weight = weight_ref[:1]

        for turn in range(inner - 1):
            away = turn + 1 + (turn + 1) // (inner // 2)
            to = lax.rem(place_ref[0] + away, inner)

            def block(z):
                at = pl.ds(pl.multiple_of(order_ref[z * inner + to] * cols, cols), cols)
                own = grad_ref[:, at].astype(jnp.float32) * own_weight
                extra = o_grad_ref[:, at].astype(jnp.float32) * factors[0]
                return jnp.concatenate([own.astype(jnp.bfloat16), extra.astype(jnp.bfloat16)], axis=0)

            for first in range(0, outer, 2):
                both = jnp.concatenate([block(first), block(first + 1)], axis=1)
                term = jnp.dot(hidden_ref[...], both, preferred_element_type=jnp.float32)
                for k in range(2):
                    ring_ref[turn, first + k] = term[:, k * cols : (k + 1) * cols]

    return pl.pallas_call(
        kernel,
        name="other_terms",
        out_shape=(
            jax.ShapeDtypeStruct((inner - 1, outer, rows, cols), jnp.float32),
            jax.ShapeDtypeStruct((3, cols), jnp.float32),
            jax.ShapeDtypeStruct((1, 1), jnp.float32),
            jax.ShapeDtypeStruct((orphans, cols), jnp.float32),
            jax.ShapeDtypeStruct((orphans, cols), jnp.float32),
        ),
        in_specs=[SMEM] * 3 + [VMEM] * 4,
        out_specs=(VMEM,) * 5,
        compiler_params=room(20),
        cost_estimate=pl.CostEstimate(
            flops=2 * rows * hidden.shape[1] * grad.shape[1],
            bytes_accessed=2 * hidden.shape[1] * grad.shape[1] + 4 * rows * grad.shape[1],
            transcendentals=0,
        ),
    )(order, place, me, names, hidden, grad, o_grad)


def ring_sum(away, blocks, ring, received, first=None):
    inner, outer, rows, cols = ring.shape[0] + 1, *ring.shape[1:]
    at = (away - 1 - away // (inner // 2)) % inner if away else inner - 2
    base, count = blocks
    operands = [a for a, _ in received]
    operands += [] if first is None else [first[0], first[2]]

    def kernel(ring_ref, *refs):
        came, (out_ref, own_ref, sem) = refs[: len(operands)], refs[len(operands) :]
        copy = pltpu.make_async_copy(ring_ref.at[at, pl.ds(base, count)], own_ref, sem)
        copy.start()
        if first is not None:
            message, weight_ref, factor_ref = came
            offset = received[0][1]
            orphans = factor_ref.shape[0]
            own = message.shape[1] - 2 * orphans
            pieces = [message[offset + z, own + orphans :] for z in range(outer // 2)]
            theirs = jnp.concatenate(pieces, axis=1).astype(jnp.float32).T
            theirs = theirs[:own].astype(jnp.bfloat16)
        copy.wait()
        for z in range(count):
            if first is None:
                total = own_ref[z]
                for c, (_, offset) in zip(came, received):
                    total = total + c[offset + z].astype(jnp.float32)
                out_ref[z] = total.astype(jnp.bfloat16)
                continue
            _, row, _, start = first
            block = message.at[offset + z]
            scaled = block[own : own + orphans].astype(jnp.float32) * factor_ref[...]
            part = block[:own].astype(jnp.float32) * weight_ref[row : row + 1]
            part = part + jnp.dot(
                theirs, scaled.astype(jnp.bfloat16), preferred_element_type=jnp.float32
            )
            out_ref[z] = own_ref[z].astype(jnp.bfloat16)
            part = own_ref[z, start : start + own] + part
            out_ref[z, start : start + own] = part.astype(jnp.bfloat16)

    return pl.pallas_call(
        kernel,
        out_shape=jax.ShapeDtypeStruct((count, rows, cols), jnp.bfloat16),
        in_specs=[pl.BlockSpec(memory_space=pl.ANY)] + [VMEM] * len(operands),
        out_specs=VMEM,
        scratch_shapes=[pltpu.VMEM((count, rows, cols), jnp.float32), pltpu.SemaphoreType.DMA],
        compiler_params=room(6),
        cost_estimate=pl.CostEstimate(
            flops=2 * count * rows * cols,
            bytes_accessed=8 * count * rows * cols,
            transcendentals=0,
        ),
    )(ring, *operands)


def near_sum(ring, *received):
    outer, rows, cols = ring.shape[1:]

    def kernel(ring_ref, *refs):
        came, (out_ref, own_ref, sem) = refs[: len(received)], refs[len(received) :]
        copy = pltpu.make_async_copy(ring_ref.at[ring.shape[0] - 1], own_ref, sem)
        copy.start()
        copy.wait()
        for z in range(outer):
            total, at = own_ref[z], 0
            for c in came:
                first = at % outer
                if first <= z < first + c.shape[0]:
                    total = total + c[z - first].astype(jnp.float32)
                at += c.shape[0]
            out_ref[z] = total.astype(jnp.bfloat16)

    return pl.pallas_call(
        kernel,
        name="near",
        out_shape=jax.ShapeDtypeStruct((outer, rows, cols), jnp.bfloat16),
        in_specs=[pl.BlockSpec(memory_space=pl.ANY)] + [VMEM] * len(received),
        out_specs=VMEM,
        scratch_shapes=[pltpu.VMEM((outer, rows, cols), jnp.float32), pltpu.SemaphoreType.DMA],
        compiler_params=room(6),
        cost_estimate=pl.CostEstimate(
            flops=2 * outer * rows * cols,
            bytes_accessed=8 * outer * rows * cols,
            transcendentals=0,
        ),
    )(ring, *received)


def total_of(near):
    outer, rows, cols = near.shape

    def kernel(near_ref, out_ref):
        whole = near_ref[0].astype(jnp.float32)
        for k in range(1, outer):
            whole = whole + near_ref[k].astype(jnp.float32)
        out_ref[...] = whole

    return pl.pallas_call(
        kernel,
        name="total_of",
        out_shape=jax.ShapeDtypeStruct((rows, cols), jnp.float32),
        in_specs=[VMEM],
        out_specs=VMEM,
        compiler_params=room(4),
    )(near)


def shifted(array, by):
    size = lax.axis_size("dp_1")
    return lax.ppermute(array, "dp_1", [(i, (i + by) % size) for i in range(size)])


def exchanged(array, axis):
    return lax.all_to_all(array, axis, split_axis=0, concat_axis=0, tiled=True)


def per_device(
    local_gate,
    local_up,
    local_grad,
    orphan_gate,
    orphan_up,
    orphan_grad,
    orphan_len,
    orphan_dest,
    loop_order,
):
    replicas = lax.axis_size(DP)
    inner = lax.axis_size("dp_1")
    me = lax.axis_index(DP).astype(jnp.int32)
    line = lax.axis_index("dp_1").astype(jnp.int32).reshape(1)
    me = me.reshape(1)
    orphans = orphan_grad.shape[0]
    live = lax.broadcasted_iota(jnp.int32, (replicas, 1, orphans), 2) < orphan_len[0]
    names = jnp.broadcast_to(orphan_dest[:, 0][None, None], live.shape)
    names = jnp.where(live, names, -1).astype(jnp.float32)
    names = exchanged(names, DP)
    hidden, up, down = first_message(
        loop_order,
        line,
        local_gate,
        local_up,
        orphan_gate.T,
        orphan_up.T,
        local_grad,
        orphan_grad,
    )
    up, down = shifted(up, 1), shifted(down, -1)
    ring, weight, load, up_factor, down_factor = other_terms(
        loop_order, line, me, names.reshape(replicas, orphans), hidden, local_grad, orphan_grad
    )
    ups, downs = (weight, 1, up_factor, 0), (weight, 2, down_factor, UP_ROWS)
    count = lax.axis_size("dp_0") // 2
    bases = (0, count)
    up, down = [(up, base) for base in bases], [(down, base) for base in bases]
    for away in range(inner // 2 - 1, 0, -1):
        back = inner - away
        for k, base in enumerate(bases):
            blocks = base, count
            sent = ring_sum(away, blocks, ring, [up[k]], ups)
            up[k] = shifted(sent, 1), 0
            sent = ring_sum(back, blocks, ring, [down[k]], downs)
            down[k] = shifted(sent, -1), 0
        ups = downs = None
    near = near_sum(ring, *[a for a, _ in up], *[a for a, _ in down])
    return total_of(exchanged(near, "dp_0")), load.reshape(1)


def solution(mesh):
    torus = Mesh(mesh.devices.reshape(4, 8, mesh.shape["tensor"]), ("dp_0", "dp_1", "tensor"))

    return jax.shard_map(
        per_device,
        mesh=torus,
        in_specs=(
            P("tensor", DP),
            P("tensor", DP),
            P(DP, None),
            P("tensor", DP),
            P("tensor", DP),
            P(DP, None),
            P(DP),
            P(DP, None),
            P(),
        ),
        out_specs=(P("tensor", DP), P(DP)),
        check_vma=False,
    )
```

```python
import jax
import jax.numpy as jnp
from jax import lax
from jax.experimental import pallas as pl
from jax.experimental.pallas import tpu as pltpu
from jax.sharding import Mesh
from jax.sharding import PartitionSpec as P


DP = ("dp_0", "dp_1")
UP_ROWS = 256
SMEM = pl.BlockSpec(memory_space=pltpu.SMEM)
VMEM = pl.BlockSpec(memory_space=pltpu.VMEM)


def room(mib):
    return pltpu.CompilerParams(vmem_limit_bytes=mib * 2**20)


def hidden_of(gate, upper):
    gate = gate.astype(jnp.float32)
    return gate / (1.0 + jnp.exp(-gate)) * upper.astype(jnp.float32)


def first_message(order, place, gate, up, o_gate, o_up, grad, o_grad):
    rows, depth = gate.shape
    outer, inner = lax.axis_size("dp_0"), lax.axis_size("dp_1")
    cols = grad.shape[1] // (outer * inner)
    orphans = o_gate.shape[0]
    half, far = UP_ROWS, inner // 2

    def kernel(order_ref, place_ref, gate_ref, up_ref, o_gate_ref, o_up_ref, *refs):
        grad_refs, o_grad_refs = refs[:outer], refs[outer : 2 * outer]
        hidden_ref, *messages = refs[2 * outer :]
        hidden_ref[:, :depth] = hidden_of(gate_ref[...], up_ref[...]).astype(jnp.bfloat16)
        extra = hidden_of(o_gate_ref[...], o_up_ref[...])
        hidden_ref[:, depth:] = extra.T.astype(jnp.bfloat16)
        for first in range(0, outer, 2):
            both = jnp.concatenate([grad_refs[first][...], grad_refs[first + 1][...]], axis=1)
            term = jnp.dot(hidden_ref[:, :depth], both, preferred_element_type=jnp.float32)
            for k in range(2):
                part = term[:, k * cols : (k + 1) * cols].astype(jnp.bfloat16)
                messages[0][first + k, :half] = part[:half]
                messages[1][first + k, : rows - half] = part[half:]
        for message, start, stop in ((messages[0], 0, half), (messages[1], half, rows)):
            at = stop - start
            for z in range(outer):
                message[z, at : at + orphans] = o_grad_refs[z][...]
                left = start + z % (outer // 2) * cols
                piece = extra[:, left : min(left + cols, stop)]
                piece = piece.astype(jnp.bfloat16)
                if piece.shape[1] < cols:
                    gap = jnp.zeros((orphans, cols - piece.shape[1]), jnp.bfloat16)
                    piece = jnp.concatenate([piece, gap], axis=1)
                message[z, at + orphans :] = piece

    def column_block(height, z):
        def at(turn, order_ref, place_ref):
            return 0, order_ref[z * inner + lax.rem(place_ref[0] + far, inner)]

        return pl.BlockSpec((height, cols), at)

    def whole(*shape):
        return pl.BlockSpec(shape, lambda turn, *_: (0,) * len(shape))

    shapes = [
        (rows, depth + orphans),
        (outer, half + 2 * orphans, cols),
        (outer, rows - half + 2 * orphans, cols),
    ]
    return pl.pallas_call(
        kernel,
        name="first_message",
        out_shape=[jax.ShapeDtypeStruct(shape, jnp.bfloat16) for shape in shapes],
        grid_spec=pltpu.PrefetchScalarGridSpec(
            num_scalar_prefetch=2,
            grid=(1,),
            in_specs=[whole(*gate.shape)] * 2
            + [whole(*o_gate.shape)] * 2
            + [column_block(depth, z) for z in range(outer)]
            + [column_block(orphans, z) for z in range(outer)],
            out_specs=[whole(*shape) for shape in shapes],
        ),
        cost_estimate=pl.CostEstimate(
            flops=2 * rows * depth * outer * cols,
            bytes_accessed=8 * rows * depth,
            transcendentals=rows * depth,
        ),
    )(order, place, gate, up, o_gate, o_up, *[grad] * outer, *[o_grad] * outer)


def write_terms(aways, order_ref, place, hidden_ref, grad_ref, o_grad_ref, weight, factor, ring_ref):
    inner, outer = lax.axis_size("dp_1"), lax.axis_size("dp_0")
    cols = ring_ref.shape[-1]
    for turn, away in enumerate(aways):
        to = lax.rem(place + away, inner)

        def block(z):
            at = pl.ds(pl.multiple_of(order_ref[z * inner + to] * cols, cols), cols)
            own = grad_ref[:, at].astype(jnp.float32) * weight
            extra = o_grad_ref[:, at].astype(jnp.float32) * factor
            return jnp.concatenate([own.astype(jnp.bfloat16), extra.astype(jnp.bfloat16)], axis=0)

        for first in range(0, outer, 2):
            both = jnp.concatenate([block(first), block(first + 1)], axis=1)
            term = jnp.dot(hidden_ref[...], both, preferred_element_type=jnp.float32)
            for k in range(2):
                ring_ref[turn, first + k] = term[:, k * cols : (k + 1) * cols]


def terms_cost(shape, depth):
    count, outer, rows, cols = shape
    return pl.CostEstimate(
        flops=2 * count * outer * rows * depth * cols,
        bytes_accessed=2 * depth * count * outer * cols + 4 * count * outer * rows * cols,
        transcendentals=0,
    )


def second_terms(aways, order, place, me, names, hidden, grad, o_grad):
    rows, depth = hidden.shape
    own_rows, _ = grad.shape
    outer, inner = lax.axis_size("dp_0"), lax.axis_size("dp_1")
    replicas = outer * inner
    orphans = o_grad.shape[0]
    cols = grad.shape[1] // replicas
    shape = (len(aways), outer, rows, cols)

    def kernel(
        order_ref, place_ref, me_ref, names_ref, hidden_ref, grad_ref, o_grad_ref,
        ring_ref, weight_ref, load_ref, *factor_refs,
    ):
        names = names_ref[...].T
        lanes = lax.broadcasted_iota(jnp.int32, (orphans, replicas), 1)
        marks = lanes.astype(jnp.float32)
        taken = jnp.zeros((orphans, replicas), jnp.float32)
        for holder in range(replicas):
            taken = taken + (names[:, holder : holder + 1] == marks).astype(jnp.float32)
        taken = jnp.sum(taken, axis=0, keepdims=True)
        weights = 1.0 / (own_rows + taken)
        line = me_ref[0] - place_ref[0]
        holders = [
            me_ref[0],
            line + lax.rem(place_ref[0] + inner - 1, inner),
            line + lax.rem(place_ref[0] + 1, inner),
        ]

        def entry(row, holder):
            return jnp.sum(jnp.where(lanes[:1] == holder, row, 0.0), axis=1, keepdims=True)

        load_ref[...] = entry(taken, holders[0]) / orphans
        for k, holder in enumerate(holders):
            weight_ref[k : k + 1] = jnp.broadcast_to(entry(weights, holder), (1, cols))
            column = jnp.sum(jnp.where(lanes == holder, names, 0.0), axis=1, keepdims=True)
            factor = jnp.sum(jnp.where(column == marks, weights, 0.0), axis=1, keepdims=True)
            factor_refs[k][...] = jnp.broadcast_to(factor, (orphans, cols))
        write_terms(
            aways, order_ref, place_ref[0], hidden_ref, grad_ref, o_grad_ref,
            weight_ref[:1], factor_refs[0][...], ring_ref,
        )

    return pl.pallas_call(
        kernel,
        name="second_terms",
        out_shape=(
            jax.ShapeDtypeStruct(shape, jnp.float32),
            jax.ShapeDtypeStruct((3, cols), jnp.float32),
            jax.ShapeDtypeStruct((1, 1), jnp.float32),
            *[jax.ShapeDtypeStruct((orphans, cols), jnp.float32)] * 3,
        ),
        in_specs=[SMEM] * 3 + [VMEM] * 4,
        out_specs=(VMEM,) * 6,
        compiler_params=room(16),
        cost_estimate=terms_cost(shape, depth),
    )(order, place, me, names, hidden, grad, o_grad)


def other_terms(aways, order, place, weight, factor, hidden, grad, o_grad):
    rows, depth = hidden.shape
    shape = (len(aways), lax.axis_size("dp_0"), rows, weight.shape[1])

    def kernel(
        order_ref, place_ref, weight_ref, factor_ref, hidden_ref, grad_ref, o_grad_ref, ring_ref
    ):
        write_terms(
            aways, order_ref, place_ref[0], hidden_ref, grad_ref, o_grad_ref,
            weight_ref[:1], factor_ref[...], ring_ref,
        )

    return pl.pallas_call(
        kernel,
        name="other_terms",
        out_shape=jax.ShapeDtypeStruct(shape, jnp.float32),
        in_specs=[SMEM] * 2 + [VMEM] * 5,
        out_specs=VMEM,
        compiler_params=room(16),
        cost_estimate=terms_cost(shape, depth),
    )(order, place, weight, factor, hidden, grad, o_grad)


def ring_sum(at, ring, received, first=None):
    outer, rows, cols = ring.shape[1:]
    operands = [*received, *([] if first is None else [first[0], first[2]])]

    def kernel(ring_ref, *refs):
        came, (out_ref, own_ref, sem) = refs[: len(operands)], refs[len(operands) :]
        copy = pltpu.make_async_copy(ring_ref.at[at], own_ref, sem)
        copy.start()
        if first is not None:
            message, weight_ref, factor_ref = came
            orphans = factor_ref.shape[0]
            own = message.shape[1] - 2 * orphans
            pieces = [message[z, own + orphans :] for z in range(outer // 2)]
            theirs = jnp.concatenate(pieces, axis=1).astype(jnp.float32).T
            theirs = theirs[:own].astype(jnp.bfloat16)
        copy.wait()
        for z in range(outer):
            if first is None:
                total = own_ref[z]
                for c in came:
                    total = total + c[z].astype(jnp.float32)
                out_ref[z] = total.astype(jnp.bfloat16)
                continue
            _, row, _, start = first
            scaled = message[z, own : own + orphans].astype(jnp.float32) * factor_ref[...]
            part = message[z, :own].astype(jnp.float32) * weight_ref[row : row + 1]
            part = part + jnp.dot(
                theirs, scaled.astype(jnp.bfloat16), preferred_element_type=jnp.float32
            )
            out_ref[z] = own_ref[z].astype(jnp.bfloat16)
            part = own_ref[z, start : start + own] + part
            out_ref[z, start : start + own] = part.astype(jnp.bfloat16)

    return pl.pallas_call(
        kernel,
        out_shape=jax.ShapeDtypeStruct((outer, rows, cols), jnp.bfloat16),
        in_specs=[pl.BlockSpec(memory_space=pl.ANY)] + [VMEM] * len(operands),
        out_specs=VMEM,
        scratch_shapes=[pltpu.VMEM((outer, rows, cols), jnp.float32), pltpu.SemaphoreType.DMA],
        compiler_params=room(6),
        cost_estimate=pl.CostEstimate(
            flops=2 * outer * rows * cols,
            bytes_accessed=8 * outer * rows * cols,
            transcendentals=0,
        ),
    )(ring, *operands)


def total_of(near):
    outer, rows, cols = near.shape

    def kernel(near_ref, out_ref):
        whole = near_ref[0].astype(jnp.float32)
        for k in range(1, outer):
            whole = whole + near_ref[k].astype(jnp.float32)
        out_ref[...] = whole

    return pl.pallas_call(
        kernel,
        name="total_of",
        out_shape=jax.ShapeDtypeStruct((rows, cols), jnp.float32),
        in_specs=[VMEM],
        out_specs=VMEM,
        compiler_params=room(4),
    )(near)


def shifted(array, by):
    size = lax.axis_size("dp_1")
    return lax.ppermute(array, "dp_1", [(i, (i + by) % size) for i in range(size)])


def exchanged(array, axis):
    return lax.all_to_all(array, axis, split_axis=0, concat_axis=0, tiled=True)


def per_device(
    local_gate,
    local_up,
    local_grad,
    orphan_gate,
    orphan_up,
    orphan_grad,
    orphan_len,
    orphan_dest,
    loop_order,
):
    replicas = lax.axis_size(DP)
    inner = lax.axis_size("dp_1")
    me = lax.axis_index(DP).astype(jnp.int32)
    line = lax.axis_index("dp_1").astype(jnp.int32).reshape(1)
    me = me.reshape(1)
    orphans = orphan_grad.shape[0]
    live = lax.broadcasted_iota(jnp.int32, (replicas, 1, orphans), 2) < orphan_len[0]
    names = jnp.broadcast_to(orphan_dest[:, 0][None, None], live.shape)
    names = jnp.where(live, names, -1).astype(jnp.float32)
    names = exchanged(names, DP)
    hidden, up, down = first_message(
        loop_order,
        line,
        local_gate,
        local_up,
        orphan_gate.T,
        orphan_up.T,
        local_grad,
        orphan_grad,
    )
    up, down = shifted(up, 1), shifted(down, -1)
    far = inner // 2
    near_by = [*range(1, far - 1), *range(far + 2, inner), 0]
    second, weight, load, factor, up_factor, down_factor = second_terms(
        (far - 1, far + 1),
        loop_order,
        line,
        me,
        names.reshape(replicas, orphans),
        hidden,
        local_grad,
        orphan_grad,
    )
    ups, downs = (weight, 1, up_factor, 0), (weight, 2, down_factor, UP_ROWS)
    up = ring_sum(0, second, [up], ups)
    up = shifted(up, 1)
    down = ring_sum(1, second, [down], downs)
    down = shifted(down, -1)
    ring = other_terms(near_by, loop_order, line, weight, factor, hidden, local_grad, orphan_grad)
    for away in range(far - 2, 0, -1):
        up = ring_sum(near_by.index(away), ring, [up])
        up = shifted(up, 1)
        down = ring_sum(near_by.index(inner - away), ring, [down])
        down = shifted(down, -1)
    near = ring_sum(near_by.index(0), ring, [up, down])
    return total_of(exchanged(near, "dp_0")), load.reshape(1)


def solution(mesh):
    torus = Mesh(mesh.devices.reshape(4, 8, mesh.shape["tensor"]), ("dp_0", "dp_1", "tensor"))

    return jax.shard_map(
        per_device,
        mesh=torus,
        in_specs=(
            P("tensor", DP),
            P("tensor", DP),
            P(DP, None),
            P("tensor", DP),
            P("tensor", DP),
            P(DP, None),
            P(DP),
            P(DP, None),
            P(),
        ),
        out_specs=(P("tensor", DP), P(DP)),
        check_vma=False,
    )
```

```python
import jax
import jax.numpy as jnp
from jax import lax
from jax.experimental import pallas as pl
from jax.experimental.pallas import tpu as pltpu
from jax.sharding import Mesh
from jax.sharding import PartitionSpec as P


DP = ("dp_0", "dp_1")
UP_ROWS = 256
SMEM = pl.BlockSpec(memory_space=pltpu.SMEM)
VMEM = pl.BlockSpec(memory_space=pltpu.VMEM)


def room(mib):
    return pltpu.CompilerParams(vmem_limit_bytes=mib * 2**20)


def hidden_of(gate, upper):
    gate = gate.astype(jnp.float32)
    return gate / (1.0 + jnp.exp(-gate)) * upper.astype(jnp.float32)


def first_message(order, place, gate, up, o_gate, o_up, grad, o_grad):
    rows, depth = gate.shape
    outer, inner = lax.axis_size("dp_0"), lax.axis_size("dp_1")
    cols = grad.shape[1] // (outer * inner)
    orphans = o_gate.shape[0]
    half, far = UP_ROWS, inner // 2

    def kernel(order_ref, place_ref, gate_ref, up_ref, o_gate_ref, o_up_ref, *refs):
        grad_refs, o_grad_refs = refs[:outer], refs[outer : 2 * outer]
        hidden_ref, *messages = refs[2 * outer :]
        hidden_ref[:, :depth] = hidden_of(gate_ref[...], up_ref[...]).astype(jnp.bfloat16)
        extra = hidden_of(o_gate_ref[...], o_up_ref[...])
        hidden_ref[:, depth:] = extra.T.astype(jnp.bfloat16)
        for first in range(0, outer, 2):
            both = jnp.concatenate([grad_refs[first][...], grad_refs[first + 1][...]], axis=1)
            term = jnp.dot(hidden_ref[:, :depth], both, preferred_element_type=jnp.float32)
            for k in range(2):
                part = term[:, k * cols : (k + 1) * cols].astype(jnp.bfloat16)
                messages[0][first + k, :half] = part[:half]
                messages[1][first + k, : rows - half] = part[half:]
        for message, start, stop in ((messages[0], 0, half), (messages[1], half, rows)):
            at = stop - start
            for z in range(outer):
                message[z, at : at + orphans] = o_grad_refs[z][...]
                left = start + z % (outer // 2) * cols
                piece = extra[:, left : min(left + cols, stop)]
                piece = piece.astype(jnp.bfloat16)
                if piece.shape[1] < cols:
                    gap = jnp.zeros((orphans, cols - piece.shape[1]), jnp.bfloat16)
                    piece = jnp.concatenate([piece, gap], axis=1)
                message[z, at + orphans :] = piece

    def column_block(height, z):
        def at(turn, order_ref, place_ref):
            return 0, order_ref[z * inner + lax.rem(place_ref[0] + far, inner)]

        return pl.BlockSpec((height, cols), at)

    def whole(*shape):
        return pl.BlockSpec(shape, lambda turn, *_: (0,) * len(shape))

    shapes = [
        (rows, depth + orphans),
        (outer, half + 2 * orphans, cols),
        (outer, rows - half + 2 * orphans, cols),
    ]
    return pl.pallas_call(
        kernel,
        name="first_message",
        out_shape=[jax.ShapeDtypeStruct(shape, jnp.bfloat16) for shape in shapes],
        grid_spec=pltpu.PrefetchScalarGridSpec(
            num_scalar_prefetch=2,
            grid=(1,),
            in_specs=[whole(*gate.shape)] * 2
            + [whole(*o_gate.shape)] * 2
            + [column_block(depth, z) for z in range(outer)]
            + [column_block(orphans, z) for z in range(outer)],
            out_specs=[whole(*shape) for shape in shapes],
        ),
        cost_estimate=pl.CostEstimate(
            flops=2 * rows * depth * outer * cols,
            bytes_accessed=8 * rows * depth,
            transcendentals=rows * depth,
        ),
    )(order, place, gate, up, o_gate, o_up, *[grad] * outer, *[o_grad] * outer)


def write_terms(aways, order_ref, place, hidden_ref, own_at, o_grad_ref, weight, factor, ring_ref):
    inner, outer = lax.axis_size("dp_1"), lax.axis_size("dp_0")
    cols = ring_ref.shape[-1]
    for turn, away in enumerate(aways):
        to = lax.rem(place + away, inner)

        def block(z):
            at = pl.ds(pl.multiple_of(order_ref[z * inner + to] * cols, cols), cols)
            own = own_at(turn, z, at).astype(jnp.float32) * weight
            extra = o_grad_ref[:, at].astype(jnp.float32) * factor
            return jnp.concatenate([own.astype(jnp.bfloat16), extra.astype(jnp.bfloat16)], axis=0)

        for first in range(0, outer, 2):
            both = jnp.concatenate([block(first), block(first + 1)], axis=1)
            term = jnp.dot(hidden_ref[...], both, preferred_element_type=jnp.float32)
            for k in range(2):
                ring_ref[turn, first + k] = term[:, k * cols : (k + 1) * cols]


def terms_cost(shape, depth):
    count, outer, rows, cols = shape
    return pl.CostEstimate(
        flops=2 * count * outer * rows * depth * cols,
        bytes_accessed=2 * depth * count * outer * cols + 4 * count * outer * rows * cols,
        transcendentals=0,
    )


def second_terms(aways, order, place, me, names, hidden, grad, o_grad):
    rows, depth = hidden.shape
    own_rows, _ = grad.shape
    outer, inner = lax.axis_size("dp_0"), lax.axis_size("dp_1")
    replicas = outer * inner
    orphans = o_grad.shape[0]
    cols = grad.shape[1] // replicas
    shape = (len(aways), outer, rows, cols)
    blocks = len(aways) * outer

    def column_block(away, z):
        def at(turn, order_ref, place_ref, me_ref):
            return 0, order_ref[z * inner + lax.rem(place_ref[0] + away, inner)]

        return pl.BlockSpec((own_rows, cols), at)

    def whole(array):
        return pl.BlockSpec(array.shape, lambda turn, *_: (0,) * len(array.shape))

    def kernel(
        order_ref, place_ref, me_ref, names_ref, hidden_ref, o_grad_ref, *refs
    ):
        grad_refs, (ring_ref, weight_ref, load_ref, *factor_refs) = refs[:blocks], refs[blocks:]
        names = names_ref[...].T
        lanes = lax.broadcasted_iota(jnp.int32, (orphans, replicas), 1)
        marks = lanes.astype(jnp.float32)
        taken = jnp.zeros((orphans, replicas), jnp.float32)
        for holder in range(replicas):
            taken = taken + (names[:, holder : holder + 1] == marks).astype(jnp.float32)
        taken = jnp.sum(taken, axis=0, keepdims=True)
        weights = 1.0 / (own_rows + taken)
        line = me_ref[0] - place_ref[0]
        holders = [
            me_ref[0],
            line + lax.rem(place_ref[0] + inner - 1, inner),
            line + lax.rem(place_ref[0] + 1, inner),
        ]

        def entry(row, holder):
            return jnp.sum(jnp.where(lanes[:1] == holder, row, 0.0), axis=1, keepdims=True)

        load_ref[...] = entry(taken, holders[0]) / orphans
        for k, holder in enumerate(holders):
            weight_ref[k : k + 1] = jnp.broadcast_to(entry(weights, holder), (1, cols))
            column = jnp.sum(jnp.where(lanes == holder, names, 0.0), axis=1, keepdims=True)
            factor = jnp.sum(jnp.where(column == marks, weights, 0.0), axis=1, keepdims=True)
            factor_refs[k][...] = jnp.broadcast_to(factor, (orphans, cols))
        write_terms(
            aways, order_ref, place_ref[0], hidden_ref,
            lambda turn, z, _: grad_refs[turn * outer + z][...], o_grad_ref,
            weight_ref[:1], factor_refs[0][...], ring_ref,
        )

    out_shape = (
        jax.ShapeDtypeStruct(shape, jnp.float32),
        jax.ShapeDtypeStruct((3, cols), jnp.float32),
        jax.ShapeDtypeStruct((1, 1), jnp.float32),
        *[jax.ShapeDtypeStruct((orphans, cols), jnp.float32)] * 3,
    )
    return pl.pallas_call(
        kernel,
        name="second_terms",
        out_shape=out_shape,
        grid_spec=pltpu.PrefetchScalarGridSpec(
            num_scalar_prefetch=3,
            grid=(1,),
            in_specs=[whole(names), whole(hidden), whole(o_grad)]
            + [column_block(away, z) for away in aways for z in range(outer)],
            out_specs=[whole(out) for out in out_shape],
        ),
        compiler_params=room(48),
        cost_estimate=terms_cost(shape, depth),
    )(order, place, me, names, hidden, o_grad, *[grad] * blocks)


def other_terms(aways, order, place, weight, factor, hidden, grad, o_grad):
    rows, depth = hidden.shape
    shape = (len(aways), lax.axis_size("dp_0"), rows, weight.shape[1])

    def kernel(
        order_ref, place_ref, weight_ref, factor_ref, hidden_ref, grad_ref, o_grad_ref, ring_ref
    ):
        write_terms(
            aways, order_ref, place_ref[0], hidden_ref,
            lambda turn, z, at: grad_ref[:, at], o_grad_ref,
            weight_ref[:1], factor_ref[...], ring_ref,
        )

    return pl.pallas_call(
        kernel,
        name="other_terms",
        out_shape=jax.ShapeDtypeStruct(shape, jnp.float32),
        in_specs=[SMEM] * 2 + [VMEM] * 5,
        out_specs=VMEM,
        compiler_params=room(16),
        cost_estimate=terms_cost(shape, depth),
    )(order, place, weight, factor, hidden, grad, o_grad)


def ring_sum(at, ring, received, first=None):
    outer, rows, cols = ring.shape[1:]
    operands = [*received, *([] if first is None else [first[0], first[2]])]

    def kernel(ring_ref, *refs):
        came, (out_ref, own_ref, sem) = refs[: len(operands)], refs[len(operands) :]
        copy = pltpu.make_async_copy(ring_ref.at[at], own_ref, sem)
        copy.start()
        if first is not None:
            message, weight_ref, factor_ref = came
            orphans = factor_ref.shape[0]
            own = message.shape[1] - 2 * orphans
            pieces = [message[z, own + orphans :] for z in range(outer // 2)]
            theirs = jnp.concatenate(pieces, axis=1).astype(jnp.float32).T
            theirs = theirs[:own].astype(jnp.bfloat16)
        copy.wait()
        for z in range(outer):
            if first is None:
                total = own_ref[z]
                for c in came:
                    total = total + c[z].astype(jnp.float32)
                out_ref[z] = total.astype(jnp.bfloat16)
                continue
            _, row, _, start = first
            scaled = message[z, own : own + orphans].astype(jnp.float32) * factor_ref[...]
            part = message[z, :own].astype(jnp.float32) * weight_ref[row : row + 1]
            part = part + jnp.dot(
                theirs, scaled.astype(jnp.bfloat16), preferred_element_type=jnp.float32
            )
            out_ref[z] = own_ref[z].astype(jnp.bfloat16)
            part = own_ref[z, start : start + own] + part
            out_ref[z, start : start + own] = part.astype(jnp.bfloat16)

    return pl.pallas_call(
        kernel,
        out_shape=jax.ShapeDtypeStruct((outer, rows, cols), jnp.bfloat16),
        in_specs=[pl.BlockSpec(memory_space=pl.ANY)] + [VMEM] * len(operands),
        out_specs=VMEM,
        scratch_shapes=[pltpu.VMEM((outer, rows, cols), jnp.float32), pltpu.SemaphoreType.DMA],
        compiler_params=room(6),
        cost_estimate=pl.CostEstimate(
            flops=2 * outer * rows * cols,
            bytes_accessed=8 * outer * rows * cols,
            transcendentals=0,
        ),
    )(ring, *operands)


def total_of(near):
    outer, rows, cols = near.shape

    def kernel(near_ref, out_ref):
        whole = near_ref[0].astype(jnp.float32)
        for k in range(1, outer):
            whole = whole + near_ref[k].astype(jnp.float32)
        out_ref[...] = whole

    return pl.pallas_call(
        kernel,
        name="total_of",
        out_shape=jax.ShapeDtypeStruct((rows, cols), jnp.float32),
        in_specs=[VMEM],
        out_specs=VMEM,
        compiler_params=room(4),
    )(near)


def shifted(array, by):
    size = lax.axis_size("dp_1")
    return lax.ppermute(array, "dp_1", [(i, (i + by) % size) for i in range(size)])


def exchanged(array, axis):
    return lax.all_to_all(array, axis, split_axis=0, concat_axis=0, tiled=True)


def per_device(
    local_gate,
    local_up,
    local_grad,
    orphan_gate,
    orphan_up,
    orphan_grad,
    orphan_len,
    orphan_dest,
    loop_order,
):
    replicas = lax.axis_size(DP)
    inner = lax.axis_size("dp_1")
    me = lax.axis_index(DP).astype(jnp.int32)
    line = lax.axis_index("dp_1").astype(jnp.int32).reshape(1)
    me = me.reshape(1)
    orphans = orphan_grad.shape[0]
    live = lax.broadcasted_iota(jnp.int32, (replicas, 1, orphans), 2) < orphan_len[0]
    names = jnp.broadcast_to(orphan_dest[:, 0][None, None], live.shape)
    names = jnp.where(live, names, -1).astype(jnp.float32)
    names = exchanged(names, DP)
    hidden, up, down = first_message(
        loop_order,
        line,
        local_gate,
        local_up,
        orphan_gate.T,
        orphan_up.T,
        local_grad,
        orphan_grad,
    )
    up, down = shifted(up, 1), shifted(down, -1)
    far = inner // 2
    near_by = [*range(1, far - 1), *range(far + 2, inner), 0]
    second, weight, load, factor, up_factor, down_factor = second_terms(
        (far - 1, far + 1),
        loop_order,
        line,
        me,
        names.reshape(replicas, orphans),
        hidden,
        local_grad,
        orphan_grad,
    )
    ups, downs = (weight, 1, up_factor, 0), (weight, 2, down_factor, UP_ROWS)
    up = ring_sum(0, second, [up], ups)
    up = shifted(up, 1)
    down = ring_sum(1, second, [down], downs)
    down = shifted(down, -1)
    ring = other_terms(near_by, loop_order, line, weight, factor, hidden, local_grad, orphan_grad)
    for away in range(far - 2, 0, -1):
        up = ring_sum(near_by.index(away), ring, [up])
        up = shifted(up, 1)
        down = ring_sum(near_by.index(inner - away), ring, [down])
        down = shifted(down, -1)
    near = ring_sum(near_by.index(0), ring, [up, down])
    return total_of(exchanged(near, "dp_0")), load.reshape(1)


def solution(mesh):
    torus = Mesh(mesh.devices.reshape(4, 8, mesh.shape["tensor"]), ("dp_0", "dp_1", "tensor"))

    return jax.shard_map(
        per_device,
        mesh=torus,
        in_specs=(
            P("tensor", DP),
            P("tensor", DP),
            P(DP, None),
            P("tensor", DP),
            P("tensor", DP),
            P(DP, None),
            P(DP),
            P(DP, None),
            P(),
        ),
        out_specs=(P("tensor", DP), P(DP)),
        check_vma=False,
    )
```
